32 devices in a mesh: blk: 8 (over z, y), rep: 4 (over x, core).
Axes of the slice: x: 2, y: 2, z: 4, core: 2. Of those that a mesh axis runs over, the one named last changes fastest.
Arguments:
- embeddings: bfloat16 [1024, 256], P('blk'), may hold values from -21 to 21
- targets: float32 [128, 1024], P('rep', 'blk'), may hold values from -180 to 180
Outputs:
- solution: float32 [128, 1024], P('rep', 'blk')
- residual: float32 [128, 1024], P('rep', 'blk')
The draws below stay inside these ranges and needn't reach their ends.
All inputs are finite; a program needn't handle non-finite values.
Results may differ from the reference program's by a relative error of at most 0.0003.
Values may be sent and summed in bfloat16 or wider, within the bound.
A program may use at most 64 MiB of HBM per device.

```python
import math
import jax
import jax.numpy as jnp
from jax import lax

DIM = 256
RHS = 128
ITERS = 2
PTS_DEV = 128
POINTS = 1024
N_BLK = 8


latent_width = 16


def draw_embeddings(key, part):
    latent_key = jax.random.fold_in(key, 11)
    mixing_key = jax.random.fold_in(key, 12)
    noise_key = jax.random.fold_in(key, 13)
    latent = jnp.clip(jax.random.normal(latent_key, (POINTS, latent_width), jnp.float32), -5.0, 5.0)
    noise = jnp.clip(0.15 * jax.random.normal(noise_key, (POINTS, DIM), jnp.float32), -0.75, 0.75)
    mixing = jnp.clip(jax.random.normal(mixing_key, (latent_width, DIM), jnp.float32), -4.0, 4.0) / math.sqrt(DIM)
    return (jnp.dot(latent, mixing) + noise).astype(jnp.bfloat16)


def draw_targets(key, part):
    point_key = jax.random.fold_in(key, 21)
    column_key = jax.random.fold_in(key, 22)
    base_key = jax.random.fold_in(key, 23)
    point_place = jnp.arange(POINTS, dtype=jnp.float32) / max(POINTS - 1, 1)
    column_place = jnp.arange(RHS, dtype=jnp.float32) / max(RHS - 1, 1)
    trend = 0.5 * math.log(3.0)
    point_scale = jnp.exp(jax.random.uniform(point_key, (POINTS,), jnp.float32, 0.0, math.log(10.0)) + trend * point_place)
    column_scale = jnp.exp(jax.random.uniform(column_key, (RHS,), jnp.float32, 0.0, math.log(10.0)) + trend * column_place)
    base = jnp.clip(jax.random.normal(base_key, (RHS, POINTS), jnp.float32), -6.0, 6.0)
    return 0.1 * base * column_scale[:, None] * point_scale[None, :]


def setup_inputs(seed: int = 0) -> dict:
    key_list = jax.random.split(jax.random.key(seed), 3)
    embeddings = draw_embeddings(jax.random.fold_in(key_list[2], 71), 0)
    targets = draw_targets(jax.random.fold_in(key_list[2], 71), 0)
    return dict(embeddings=embeddings, targets=targets)


length_scale = 1.0
noise_var = 1.0

def squared_norms(points):
    widened = points.astype(jnp.float32)
    return lax.optimization_barrier(jnp.sum(widened * widened, axis=1))

def kernel_tile(own_points, own_norms, own_labels, far_points, far_norms, far_labels):
    products = jnp.einsum('pd,qd->pq', own_points, far_points, preferred_element_type=jnp.float32)
    distance_sq = own_norms[:, None] + far_norms[None, :] - 2.0 * products
    distance_sq = jnp.where(own_labels[:, None] == far_labels[None, :], 0.0, distance_sq)
    return jnp.exp(-jnp.sqrt(distance_sq) / length_scale)

def reference(embeddings, targets):
    all_norms = squared_norms(embeddings)
    all_labels = jnp.arange(POINTS, dtype=jnp.int32)

    def operate(direction):

        def one_block(block):
            begin = (block * PTS_DEV).astype(jnp.int32)
            own_points = lax.dynamic_slice_in_dim(embeddings, begin, PTS_DEV, 0)
            own_norms = lax.dynamic_slice_in_dim(all_norms, begin, PTS_DEV, 0)
            own_labels = lax.dynamic_slice_in_dim(all_labels, begin, PTS_DEV, 0)
            tile = kernel_tile(own_points, own_norms, own_labels, embeddings, all_norms, all_labels)
            return jnp.einsum('rq,pq->rp', direction, tile, precision=lax.Precision.HIGHEST, preferred_element_type=jnp.float32)
        pieces = lax.map(one_block, jnp.arange(N_BLK, dtype=jnp.int32))
        image = jnp.transpose(pieces, (1, 0, 2)).reshape(RHS, POINTS)
        return image + noise_var * direction
    solution = jnp.zeros_like(targets)
    residual = targets
    direction = targets
    norm_now = jnp.sum(residual * residual)
    for iteration in range(ITERS):
        image = operate(direction)
        alpha = norm_now / jnp.sum(direction * image)
        solution = solution + alpha * direction
        residual = residual - alpha * image
        norm_next = jnp.sum(residual * residual)
        direction = residual + norm_next / norm_now * direction
        norm_now = norm_next
    return (solution, residual)
```

```python
import functools

import jax
import jax.numpy as jnp
from jax import lax
from jax.experimental import pallas as pl
from jax.experimental.pallas import tpu as pltpu
from jax.sharding import PartitionSpec as P

ITERS = 2
MESH = pl.DeviceIdType.MESH
TINY = 1e-30

length_scale = 1.0
noise_var = 1.0


def flip(index, mask):
    bit = 1
    while bit <= mask:
        if mask & bit:
            index = index + bit * (1 - 2 * ((index // bit) % 2))
        bit *= 2
    return index


def dot_nt(a, b):
    return lax.dot_general(a, b, (((1,), (1,)), ((), ())), preferred_element_type=jnp.float32)


def split(x):
    high = x.astype(jnp.bfloat16)
    low = (x - high.astype(jnp.float32)).astype(jnp.bfloat16)
    return high, low


def product(v_ref, high_ref, low_ref, rhs, rows, columns):
    both = jnp.dot(v_ref[:, rows], high_ref[rows, columns], preferred_element_type=jnp.float32)
    low = jnp.dot(v_ref[pl.ds(0, rhs), rows], low_ref[rows, columns], preferred_element_type=jnp.float32)
    return both[:rhs] + (both[rhs:] + low)


def fold(x):
    rows = jnp.sum(x, axis=0, keepdims=True)
    total = rows[:, :128]
    for at in range(128, rows.shape[1], 128):
        total = total + rows[:, at : at + 128]
    return total


def kernel(
    n_blk,
    n_rep,
    emb_hbm,
    tgt_hbm,
    out_ref,
    emb,
    tgt,
    scaled,
    col_norm,
    row_norm,
    k_high,
    k_low,
    v_pair,
    image,
    parts,
    load_sem,
    emb_send,
    emb_recv,
    tgt_send,
    tgt_recv,
    core_send,
    core_recv,
    part_send,
    part_recv,
):
    pts, dim = emb.shape[2] * 2, emb.shape[3]
    rhs = tgt.shape[1]
    me = lax.axis_index("blk")
    rep = lax.axis_index("rep")
    half = rep % 2
    masks = [0, 1] + list(range(2, n_blk, 2)) + list(range(3, n_blk, 2))
    place = {mask: p for p, mask in enumerate(masks)}
    direct = [1] + list(range(2, n_blk, 2))

    loads = [
        pltpu.make_async_copy(emb_hbm.at[pl.ds(i * (pts // 2), pts // 2)], emb.at[0, i], load_sem.at[i])
        for i in range(2)
    ] + [pltpu.make_async_copy(tgt_hbm, tgt.at[0], load_sem.at[2])]
    for load in loads:
        load.start()

    barrier = pltpu.get_barrier_semaphore()
    for mask in direct:
        pl.semaphore_signal(barrier, inc=1, device_id=(flip(me, mask), rep), device_id_type=MESH)
    for mask in range(1, n_rep):
        pl.semaphore_signal(barrier, inc=1, device_id=(me, flip(rep, mask)), device_id_type=MESH)
    for load in loads:
        load.wait()
    pl.semaphore_wait(barrier, len(direct) + n_rep - 1)

    def send_emb(source, target, to):
        return pltpu.make_async_remote_copy(
            src_ref=emb.at[source, half],
            dst_ref=emb.at[target, half],
            send_sem=emb_send.at[target],
            recv_sem=emb_recv.at[target],
            device_id=(flip(me, to), rep),
            device_id_type=MESH,
        )

    def send_tgt(source, target, to):
        return pltpu.make_async_remote_copy(
            src_ref=tgt.at[source],
            dst_ref=tgt.at[target],
            send_sem=tgt_send.at[target],
            recv_sem=tgt_recv.at[target],
            device_id=(flip(me, to), rep),
            device_id_type=MESH,
        )

    def send_core(at):
        return pltpu.make_async_remote_copy(
            src_ref=emb.at[at, half],
            dst_ref=emb.at[at, half],
            send_sem=core_send.at[at],
            recv_sem=core_recv.at[at],
            device_id=(me, flip(rep, 1)),
            device_id_type=MESH,
        )

    emb_copies, tgt_copies, core_copies = {}, {}, {}
    for mask in sorted(direct, reverse=True):
        p = place[mask]
        emb_copies[p] = send_emb(0, p, mask)
        emb_copies[p].start()
    for mask in sorted(direct, reverse=True):
        p = place[mask]
        tgt_copies[p] = send_tgt(0, p, mask)
        tgt_copies[p].start()

    def arrive(p):
        mask = masks[p]
        onward = place[mask + 1] if mask >= 2 and mask % 2 == 0 else None
        if onward is not None:
            emb_copies[onward] = send_emb(p, onward, 1)
            tgt_copies[onward] = send_tgt(p, onward, 1)
        emb_copies[p].wait_recv()
        core_copies[p] = send_core(p)
        core_copies[p].start()
        if onward is not None:
            emb_copies[onward].start()
        tgt_copies[p].wait_recv()
        if onward is not None:
            tgt_copies[onward].start()

    def tile(own, own_norm, far, far_norm):
        distance = jnp.maximum((own_norm + far_norm) + dot_nt(own, far), TINY)
        return jnp.exp(-(distance * lax.rsqrt(distance)) / length_scale)

    ones = jnp.ones((8, dim), jnp.bfloat16)

    def build(p):
        here = pl.ds(p * pts, pts)
        points = emb[p].reshape(pts, dim)
        wide = points.astype(jnp.float32)
        squares = wide * wide
        col_norm[here, :] = jnp.sum(squares, axis=1, keepdims=True)
        s_high, s_low = split(squares)
        row_norm[:, here] = dot_nt(ones, s_high) + dot_nt(ones, s_low)
        scaled[here, :] = -2.0 * points
        v_high, v_low = split(tgt[p])
        v_pair[pl.ds(0, rhs), here] = v_high
        v_pair[pl.ds(rhs, rhs), here] = v_low
        upto, before = pl.ds(0, (p + 1) * pts), pl.ds(0, p * pts)
        far = emb[0 : p + 1].reshape((p + 1) * pts, dim)
        for_row = tile(scaled[here, :], col_norm[here, :], far, row_norm[0:1, upto])
        diagonal = for_row[:, p * pts :]
        row_id = lax.broadcasted_iota(jnp.int32, (pts, pts), 0)
        col_id = lax.broadcasted_iota(jnp.int32, (pts, pts), 1)
        d_high, d_low = split(jnp.where(row_id == col_id, 1.0, diagonal))
        k_high[here, here] = d_high
        k_low[here, here] = d_low
        if p:
            r_high, r_low = split(for_row[:, : p * pts])
            k_high[here, before] = r_high
            k_low[here, before] = r_low
            for_col = tile(scaled[before, :], col_norm[before, :], points, row_norm[0:1, here])
            c_high, c_low = split(for_col)
            k_high[before, here] = c_high
            k_low[before, here] = c_low
            image[:, before] += product(v_pair, k_high, k_low, rhs, here, before)
        image[:, here] = product(v_pair, k_high, k_low, rhs, upto, here)

    build(0)
    last_direct = len(direct)
    for p in range(1, n_blk):
        arrive(p)
        core_copies[p].wait_recv()
        build(p)

    everything = jnp.concatenate([tgt[p] for p in range(n_blk)], axis=1)
    along = image[...] + noise_var * everything
    rr, pr = fold(everything * everything), fold(everything * along)
    rr_sum = jnp.sum(rr, axis=1, keepdims=True)
    pr_sum = jnp.sum(pr, axis=1, keepdims=True)

    def step_of(norm, prod):
        usable = jnp.logical_and(norm > 0.0, prod > 0.0)
        return jnp.where(usable, norm / jnp.where(usable, prod, 1.0), 1.0)

    local = step_of(rr_sum, pr_sum)
    w = everything - local * along
    w_high, w_low = split(w)
    v_pair[pl.ds(0, rhs), :] = w_high
    v_pair[pl.ds(rhs, rhs), :] = w_low
    whole = pl.ds(0, n_blk * pts)
    aw = product(v_pair, k_high, k_low, rhs, whole, whole) + noise_var * w
    aa = (along - aw) / local
    sums = jnp.concatenate(
        [
            rr,
            pr,
            fold(w * w),
            fold(w * along),
            fold(along * along),
            fold(w * aw),
            fold(w * aa + along * aw),
            fold(along * aa),
        ],
        axis=0,
    )
    parts[0] = jnp.broadcast_to(jnp.sum(sums, axis=1, keepdims=True), parts.shape[1:])
    part_copies = []
    for mask in range(1, n_rep):
        copy = pltpu.make_async_remote_copy(
            src_ref=parts.at[0],
            dst_ref=parts.at[mask],
            send_sem=part_send.at[mask],
            recv_sem=part_recv.at[mask],
            device_id=(me, flip(rep, mask)),
            device_id_type=MESH,
        )
        copy.start()
        part_copies.append(copy)
    for p in range(1, n_blk):
        emb_copies[p].wait_send()
        tgt_copies[p].wait_send()
        core_copies[p].wait_send()
    for copy in part_copies:
        copy.wait()

    tiles = [parts[i] for i in range(n_rep)]
    norm_now = sum(t[0:1] for t in tiles)
    alpha = norm_now / sum(t[1:2] for t in tiles)
    norm_next = jnp.zeros_like(norm_now)
    prod = jnp.zeros_like(norm_now)
    for t in tiles:
        delta = alpha - step_of(t[0:1], t[1:2])
        norm_next = norm_next + (t[2:3] - delta * (2.0 * t[3:4] - delta * t[4:5]))
        prod = prod + (t[5:6] - delta * (t[6:7] - delta * t[7:8]))
    ratio = norm_next / norm_now
    alpha_next = norm_next / (prod - ratio * norm_next / alpha)
    delta = alpha - step_of(tiles[0][0:1], tiles[0][1:2])
    own_t, own_a = everything[:, :pts], along[:, :pts]
    residual = w[:, :pts] - delta * own_a
    image_r = aw[:, :pts] - delta * aa[:, :pts]
    direction = residual + ratio * own_t
    out_ref[0] = alpha * own_t + alpha_next * direction
    out_ref[1] = residual - alpha_next * (image_r + ratio * own_a)


def fused(n_blk, n_rep, embeddings, targets):
    pts, dim = embeddings.shape
    rhs = targets.shape[0]
    total = n_blk * pts
    dma = pltpu.SemaphoreType.DMA
    out = pl.pallas_call(
        functools.partial(kernel, n_blk, n_rep),
        out_shape=jax.ShapeDtypeStruct((2, rhs, pts), jnp.float32),
        in_specs=[pl.BlockSpec(memory_space=pl.ANY)] * 2,
        out_specs=pl.BlockSpec(memory_space=pltpu.VMEM),
        scratch_shapes=[
            pltpu.VMEM((n_blk, 2, pts // 2, dim), jnp.bfloat16),
            pltpu.VMEM((n_blk, rhs, pts), jnp.float32),
            pltpu.VMEM((total, dim), jnp.bfloat16),
            pltpu.VMEM((total, 1), jnp.float32),
            pltpu.VMEM((8, total), jnp.float32),
            pltpu.VMEM((total, total), jnp.bfloat16),
            pltpu.VMEM((total, total), jnp.bfloat16),
            pltpu.VMEM((2 * rhs, total), jnp.bfloat16),
            pltpu.VMEM((rhs, total), jnp.float32),
            pltpu.VMEM((n_rep, 8, 128), jnp.float32),
            dma((3,)),
            dma((n_blk,)),
            dma((n_blk,)),
            dma((n_blk,)),
            dma((n_blk,)),
            dma((n_blk,)),
            dma((n_blk,)),
            dma((n_rep,)),
            dma((n_rep,)),
        ],
        compiler_params=pltpu.CompilerParams(collective_id=0, has_side_effects=True),
    )(embeddings, targets)
    return out[0], out[1]


def power_of_two(n):
    return n >= 2 and n & (n - 1) == 0


def fits(n_blk, n_rep, embeddings, targets):
    pts, dim = embeddings.shape
    rhs = targets.shape[0]
    total = n_blk * pts
    return (
        power_of_two(n_blk)
        and power_of_two(n_rep)
        and pts == 128
        and dim % 128 == 0
        and rhs % 16 == 0
        and rhs <= 128
        and total <= 2048
        and dim <= 1024
    )


def squared_norms(points):
    widened = points.astype(jnp.float32)
    return jnp.sum(widened * widened, axis=1)


def kernel_tile(own_points, own_norms, own_labels, far_points, far_norms, far_labels):
    products = jnp.einsum("pd,qd->pq", own_points, far_points, preferred_element_type=jnp.float32)
    distance_sq = own_norms[:, None] + far_norms[None, :] - 2.0 * products
    distance_sq = jnp.where(own_labels[:, None] == far_labels[None, :], 0.0, distance_sq)
    return jnp.exp(-jnp.sqrt(distance_sq) / length_scale)


def paired(residual, image):
    return lax.psum((jnp.sum(residual * residual), jnp.sum(residual * image)), ("blk", "rep"))


def per_device(embeddings, targets):
    block_id = lax.axis_index("blk")
    local_count = embeddings.shape[0]
    own_norms = squared_norms(embeddings)
    own_labels = block_id * local_count + jnp.arange(local_count, dtype=jnp.int32)
    everyone = lax.all_gather(embeddings, "blk", axis=0, tiled=True)
    every_norms = squared_norms(everyone)

    def folded_image(direction):
        piece = lax.all_gather(direction, "blk", axis=1, tiled=True)
        count = piece.shape[1]
        far_labels = jnp.arange(count, dtype=jnp.int32)
        tile = kernel_tile(embeddings, own_norms, own_labels, everyone, every_norms, far_labels)
        total = jnp.einsum(
            "rq,pq->rp",
            piece,
            tile,
            precision=lax.Precision.HIGHEST,
            preferred_element_type=jnp.float32,
        )
        return total + noise_var * direction

    solution = jnp.zeros_like(targets)
    residual = targets
    image = folded_image(residual)
    norm_now, product = paired(residual, image)
    alpha = norm_now / product
    direction = residual
    along = image
    for iteration in range(ITERS):
        solution = solution + alpha * direction
        residual = residual - alpha * along
        if iteration + 1 < ITERS:
            image = folded_image(residual)
            norm_next, product = paired(residual, image)
            ratio = norm_next / norm_now
            alpha = norm_next / (product - ratio * norm_next / alpha)
            direction = residual + ratio * direction
            along = image + ratio * along
            norm_now = norm_next
    return (solution, residual)


def solution(mesh):
    n_blk, n_rep = mesh.shape["blk"], mesh.shape["rep"]

    def step(embeddings, targets):
        if fits(n_blk, n_rep, embeddings, targets):
            return fused(n_blk, n_rep, embeddings, targets)
        return per_device(embeddings, targets)

    in_specs = (P("blk", None), P("rep", "blk"))
    out_specs = (P("rep", "blk"), P("rep", "blk"))
    return jax.shard_map(step, mesh=mesh, in_specs=in_specs, out_specs=out_specs, check_vma=False)
```

```python
import functools

import jax
import jax.numpy as jnp
from jax import lax
from jax.experimental import pallas as pl
from jax.experimental.pallas import tpu as pltpu
from jax.sharding import PartitionSpec as P

ITERS = 2
MESH = pl.DeviceIdType.MESH
TINY = 1e-30

length_scale = 1.0
noise_var = 1.0


def flip(index, mask):
    bit = 1
    while bit <= mask:
        if mask & bit:
            index = index + bit * (1 - 2 * ((index // bit) % 2))
        bit *= 2
    return index


def dot_nt(a, b):
    return lax.dot_general(a, b, (((1,), (1,)), ((), ())), preferred_element_type=jnp.float32)


def split(x):
    high = x.astype(jnp.bfloat16)
    low = (x - high.astype(jnp.float32)).astype(jnp.bfloat16)
    return high, low


def product(v_ref, high_ref, low_ref, rhs, rows, columns):
    both = jnp.dot(v_ref[:, rows], high_ref[rows, columns], preferred_element_type=jnp.float32)
    low = jnp.dot(v_ref[pl.ds(0, rhs), rows], low_ref[rows, columns], preferred_element_type=jnp.float32)
    return both[:rhs] + (both[rhs:] + low)


def fold(x):
    rows = jnp.sum(x, axis=0, keepdims=True)
    total = rows[:, :128]
    for at in range(128, rows.shape[1], 128):
        total = total + rows[:, at : at + 128]
    return total


def kernel(
    n_blk,
    n_rep,
    emb_hbm,
    tgt_hbm,
    out_ref,
    emb,
    tgt,
    scaled,
    col_norm,
    row_norm,
    k_high,
    k_low,
    v_pair,
    parts,
    load_sem,
    emb_send,
    emb_recv,
    tgt_send,
    tgt_recv,
    core_send,
    core_recv,
    part_send,
    part_recv,
):
    pts, dim = emb.shape[2] * 2, emb.shape[3]
    rhs = tgt.shape[1]
    me = lax.axis_index("blk")
    rep = lax.axis_index("rep")
    half = rep % 2
    masks = [0, 1] + list(range(2, n_blk, 2)) + list(range(3, n_blk, 2))
    place = {mask: p for p, mask in enumerate(masks)}
    direct = [1] + list(range(2, n_blk, 2))

    loads = [
        pltpu.make_async_copy(emb_hbm.at[pl.ds(i * (pts // 2), pts // 2)], emb.at[0, i], load_sem.at[i])
        for i in range(2)
    ] + [pltpu.make_async_copy(tgt_hbm, tgt.at[0], load_sem.at[2])]
    for load in loads:
        load.start()

    barrier = pltpu.get_barrier_semaphore()
    for mask in direct:
        pl.semaphore_signal(barrier, inc=1, device_id=(flip(me, mask), rep), device_id_type=MESH)
    for mask in range(1, n_rep):
        pl.semaphore_signal(barrier, inc=1, device_id=(me, flip(rep, mask)), device_id_type=MESH)
    for load in loads:
        load.wait()
    pl.semaphore_wait(barrier, len(direct) + n_rep - 1)

    def send_emb(source, target, to):
        return pltpu.make_async_remote_copy(
            src_ref=emb.at[source, half],
            dst_ref=emb.at[target, half],
            send_sem=emb_send.at[target],
            recv_sem=emb_recv.at[target],
            device_id=(flip(me, to), rep),
            device_id_type=MESH,
        )

    def send_tgt(source, target, to):
        return pltpu.make_async_remote_copy(
            src_ref=tgt.at[source],
            dst_ref=tgt.at[target],
            send_sem=tgt_send.at[target],
            recv_sem=tgt_recv.at[target],
            device_id=(flip(me, to), rep),
            device_id_type=MESH,
        )

    def send_core(at):
        return pltpu.make_async_remote_copy(
            src_ref=emb.at[at, half],
            dst_ref=emb.at[at, half],
            send_sem=core_send.at[at],
            recv_sem=core_recv.at[at],
            device_id=(me, flip(rep, 1)),
            device_id_type=MESH,
        )

    emb_copies, tgt_copies, core_copies = {}, {}, {}
    for mask in sorted(direct, reverse=True):
        p = place[mask]
        emb_copies[p] = send_emb(0, p, mask)
        emb_copies[p].start()
    for mask in sorted(direct, reverse=True):
        p = place[mask]
        tgt_copies[p] = send_tgt(0, p, mask)
        tgt_copies[p].start()

    def take_emb(p):
        onward = place[masks[p] + 1] if masks[p] in direct[1:] else None
        emb_copies[p].wait_recv()
        core_copies[p] = send_core(p)
        core_copies[p].start()
        if onward is not None:
            emb_copies[onward] = send_emb(p, onward, 1)
            emb_copies[onward].start()

    def take_tgt(p):
        onward = place[masks[p] + 1] if masks[p] in direct[1:] else None
        tgt_copies[p].wait_recv()
        if onward is not None:
            tgt_copies[onward] = send_tgt(p, onward, 1)
            tgt_copies[onward].start()

    def tile(own, own_norm, far, far_norm):
        distance = jnp.maximum((own_norm + far_norm) + dot_nt(own, far), TINY)
        return jnp.exp(-(distance * lax.rsqrt(distance)) / length_scale)

    ones = jnp.ones((8, dim), jnp.bfloat16)

    def build(p):
        here = pl.ds(p * pts, pts)
        points = emb[p].reshape(pts, dim)
        wide = points.astype(jnp.float32)
        squares = wide * wide
        col_norm[here, :] = jnp.sum(squares, axis=1, keepdims=True)
        s_high, s_low = split(squares)
        row_norm[:, here] = dot_nt(ones, s_high) + dot_nt(ones, s_low)
        scaled[here, :] = -2.0 * points
        upto, before = pl.ds(0, (p + 1) * pts), pl.ds(0, p * pts)
        far = emb[0 : p + 1].reshape((p + 1) * pts, dim)
        for_row = tile(scaled[here, :], col_norm[here, :], far, row_norm[0:1, upto])
        diagonal = for_row[:, p * pts :]
        row_id = lax.broadcasted_iota(jnp.int32, (pts, pts), 0)
        col_id = lax.broadcasted_iota(jnp.int32, (pts, pts), 1)
        d_high, d_low = split(jnp.where(row_id == col_id, 1.0, diagonal))
        k_high[here, here] = d_high
        k_low[here, here] = d_low
        if p:
            r_high, r_low = split(for_row[:, : p * pts])
            k_high[here, before] = r_high
            k_low[here, before] = r_low
            for_col = tile(scaled[before, :], col_norm[before, :], points, row_norm[0:1, here])
            c_high, c_low = split(for_col)
            k_high[before, here] = c_high
            k_low[before, here] = c_low

    build(0)
    n_direct = len(direct)

    def add(p):
        core_copies[p].wait_recv()
        build(p)

    for p in range(1, n_direct + 1):
        take_emb(p)
    for p in range(1, n_direct):
        add(p)
    for p in range(1, n_direct + 1):
        take_tgt(p)
    if n_direct + 1 < n_blk:
        take_emb(n_direct + 1)
    add(n_direct)
    for p in range(n_direct + 2, n_blk):
        take_emb(p)
    for p in range(n_direct + 1, n_blk):
        add(p)
    for p in range(n_direct + 1, n_blk):
        take_tgt(p)

    whole = pl.ds(0, n_blk * pts)

    def apply(v):
        v_high, v_low = split(v)
        v_pair[pl.ds(0, rhs), :] = v_high
        v_pair[pl.ds(rhs, rhs), :] = v_low
        return product(v_pair, k_high, k_low, rhs, whole, whole) + noise_var * v

    everything = jnp.concatenate([tgt[p] for p in range(n_blk)], axis=1)
    along = apply(everything)
    rr, pr = fold(everything * everything), fold(everything * along)
    rr_sum = jnp.sum(rr, axis=1, keepdims=True)
    pr_sum = jnp.sum(pr, axis=1, keepdims=True)

    def step_of(norm, prod):
        usable = jnp.logical_and(norm > 0.0, prod > 0.0)
        return jnp.where(usable, norm / jnp.where(usable, prod, 1.0), 1.0)

    local = step_of(rr_sum, pr_sum)
    w = everything - local * along
    aw = apply(w)
    aa = (along - aw) / local
    sums = jnp.concatenate(
        [
            rr,
            pr,
            fold(w * w),
            fold(w * along),
            fold(along * along),
            fold(w * aw),
            fold(w * aa + along * aw),
            fold(along * aa),
        ],
        axis=0,
    )
    parts[0] = jnp.broadcast_to(jnp.sum(sums, axis=1, keepdims=True), parts.shape[1:])
    part_copies = []
    for mask in range(1, n_rep):
        copy = pltpu.make_async_remote_copy(
            src_ref=parts.at[0],
            dst_ref=parts.at[mask],
            send_sem=part_send.at[mask],
            recv_sem=part_recv.at[mask],
            device_id=(me, flip(rep, mask)),
            device_id_type=MESH,
        )
        copy.start()
        part_copies.append(copy)
    for p in range(1, n_blk):
        emb_copies[p].wait_send()
        tgt_copies[p].wait_send()
        core_copies[p].wait_send()
    for copy in part_copies:
        copy.wait()

    tiles = [parts[i] for i in range(n_rep)]
    norm_now = sum(t[0:1] for t in tiles)
    alpha = norm_now / sum(t[1:2] for t in tiles)
    norm_next = jnp.zeros_like(norm_now)
    prod = jnp.zeros_like(norm_now)
    for t in tiles:
        delta = alpha - step_of(t[0:1], t[1:2])
        norm_next = norm_next + (t[2:3] - delta * (2.0 * t[3:4] - delta * t[4:5]))
        prod = prod + (t[5:6] - delta * (t[6:7] - delta * t[7:8]))
    ratio = norm_next / norm_now
    alpha_next = norm_next / (prod - ratio * norm_next / alpha)
    delta = alpha - step_of(tiles[0][0:1], tiles[0][1:2])
    own_t, own_a = everything[:, :pts], along[:, :pts]
    residual = w[:, :pts] - delta * own_a
    image_r = aw[:, :pts] - delta * aa[:, :pts]
    direction = residual + ratio * own_t
    out_ref[0] = alpha * own_t + alpha_next * direction
    out_ref[1] = residual - alpha_next * (image_r + ratio * own_a)


def fused(n_blk, n_rep, embeddings, targets):
    pts, dim = embeddings.shape
    rhs = targets.shape[0]
    total = n_blk * pts
    dma = pltpu.SemaphoreType.DMA
    out = pl.pallas_call(
        functools.partial(kernel, n_blk, n_rep),
        out_shape=jax.ShapeDtypeStruct((2, rhs, pts), jnp.float32),
        in_specs=[pl.BlockSpec(memory_space=pl.ANY)] * 2,
        out_specs=pl.BlockSpec(memory_space=pltpu.VMEM),
        scratch_shapes=[
            pltpu.VMEM((n_blk, 2, pts // 2, dim), jnp.bfloat16),
            pltpu.VMEM((n_blk, rhs, pts), jnp.float32),
            pltpu.VMEM((total, dim), jnp.bfloat16),
            pltpu.VMEM((total, 1), jnp.float32),
            pltpu.VMEM((8, total), jnp.float32),
            pltpu.VMEM((total, total), jnp.bfloat16),
            pltpu.VMEM((total, total), jnp.bfloat16),
            pltpu.VMEM((2 * rhs, total), jnp.bfloat16),
            pltpu.VMEM((n_rep, 8, 128), jnp.float32),
            dma((3,)),
            dma((n_blk,)),
            dma((n_blk,)),
            dma((n_blk,)),
            dma((n_blk,)),
            dma((n_blk,)),
            dma((n_blk,)),
            dma((n_rep,)),
            dma((n_rep,)),
        ],
        compiler_params=pltpu.CompilerParams(collective_id=0, has_side_effects=True),
    )(embeddings, targets)
    return out[0], out[1]


def power_of_two(n):
    return n >= 2 and n & (n - 1) == 0


def fits(n_blk, n_rep, embeddings, targets):
    pts, dim = embeddings.shape
    rhs = targets.shape[0]
    total = n_blk * pts
    return (
        power_of_two(n_blk)
        and power_of_two(n_rep)
        and pts == 128
        and dim % 128 == 0
        and rhs % 16 == 0
        and rhs <= 128
        and total <= 2048
        and dim <= 1024
    )


def squared_norms(points):
    widened = points.astype(jnp.float32)
    return jnp.sum(widened * widened, axis=1)


def kernel_tile(own_points, own_norms, own_labels, far_points, far_norms, far_labels):
    products = jnp.einsum("pd,qd->pq", own_points, far_points, preferred_element_type=jnp.float32)
    distance_sq = own_norms[:, None] + far_norms[None, :] - 2.0 * products
    distance_sq = jnp.where(own_labels[:, None] == far_labels[None, :], 0.0, distance_sq)
    return jnp.exp(-jnp.sqrt(distance_sq) / length_scale)


def paired(residual, image):
    return lax.psum((jnp.sum(residual * residual), jnp.sum(residual * image)), ("blk", "rep"))


def per_device(embeddings, targets):
    block_id = lax.axis_index("blk")
    local_count = embeddings.shape[0]
    own_norms = squared_norms(embeddings)
    own_labels = block_id * local_count + jnp.arange(local_count, dtype=jnp.int32)
    everyone = lax.all_gather(embeddings, "blk", axis=0, tiled=True)
    every_norms = squared_norms(everyone)

    def folded_image(direction):
        piece = lax.all_gather(direction, "blk", axis=1, tiled=True)
        count = piece.shape[1]
        far_labels = jnp.arange(count, dtype=jnp.int32)
        tile = kernel_tile(embeddings, own_norms, own_labels, everyone, every_norms, far_labels)
        total = jnp.einsum(
            "rq,pq->rp",
            piece,
            tile,
            precision=lax.Precision.HIGHEST,
            preferred_element_type=jnp.float32,
        )
        return total + noise_var * direction

    solution = jnp.zeros_like(targets)
    residual = targets
    image = folded_image(residual)
    norm_now, product = paired(residual, image)
    alpha = norm_now / product
    direction = residual
    along = image
    for iteration in range(ITERS):
        solution = solution + alpha * direction
        residual = residual - alpha * along
        if iteration + 1 < ITERS:
            image = folded_image(residual)
            norm_next, product = paired(residual, image)
            ratio = norm_next / norm_now
            alpha = norm_next / (product - ratio * norm_next / alpha)
            direction = residual + ratio * direction
            along = image + ratio * along
            norm_now = norm_next
    return (solution, residual)


def solution(mesh):
    n_blk, n_rep = mesh.shape["blk"], mesh.shape["rep"]

    def step(embeddings, targets):
        if fits(n_blk, n_rep, embeddings, targets):
            return fused(n_blk, n_rep, embeddings, targets)
        return per_device(embeddings, targets)

    in_specs = (P("blk", None), P("rep", "blk"))
    out_specs = (P("rep", "blk"), P("rep", "blk"))
    return jax.shard_map(step, mesh=mesh, in_specs=in_specs, out_specs=out_specs, check_vma=False)
```

```python
import functools

import jax
import jax.numpy as jnp
from jax import lax
from jax.experimental import pallas as pl
from jax.experimental.pallas import tpu as pltpu
from jax.sharding import PartitionSpec as P

ITERS = 2
MESH = pl.DeviceIdType.MESH
TINY = 1e-30

length_scale = 1.0
noise_var = 1.0


def flip(index, mask):
    bit = 1
    while bit <= mask:
        if mask & bit:
            index = index + bit * (1 - 2 * ((index // bit) % 2))
        bit *= 2
    return index


def dot_nt(a, b):
    return lax.dot_general(a, b, (((1,), (1,)), ((), ())), preferred_element_type=jnp.float32)


def split(x):
    high = x.astype(jnp.bfloat16)
    low = (x - high.astype(jnp.float32)).astype(jnp.bfloat16)
    return high, low


def product(v_ref, high_ref, low_ref, rhs, rows, columns):
    both = jnp.dot(v_ref[:, rows], high_ref[rows, columns], preferred_element_type=jnp.float32)
    low = jnp.dot(v_ref[pl.ds(0, rhs), rows], low_ref[rows, columns], preferred_element_type=jnp.float32)
    return both[:rhs] + (both[rhs:] + low)


def fold(x):
    rows = jnp.sum(x, axis=0, keepdims=True)
    total = rows[:, :128]
    for at in range(128, rows.shape[1], 128):
        total = total + rows[:, at : at + 128]
    return total


def kernel(
    n_blk,
    n_rep,
    emb_hbm,
    tgt_hbm,
    out_ref,
    emb,
    tgt,
    scaled,
    col_norm,
    row_norm,
    k_high,
    k_low,
    v_pair,
    parts,
    load_sem,
    emb_send,
    emb_recv,
    tgt_send,
    tgt_recv,
    core_send,
    core_recv,
    part_send,
    part_recv,
):
    pts, dim = emb.shape[2] * 2, emb.shape[3]
    rhs = tgt.shape[1]
    me = lax.axis_index("blk")
    rep = lax.axis_index("rep")
    half = rep % 2
    masks = [0, 1] + list(range(2, n_blk, 2)) + list(range(3, n_blk, 2))
    place = {mask: p for p, mask in enumerate(masks)}
    direct = [1] + list(range(2, n_blk, 2))

    loads = [
        pltpu.make_async_copy(emb_hbm.at[pl.ds(i * (pts // 2), pts // 2)], emb.at[0, i], load_sem.at[i])
        for i in range(2)
    ] + [pltpu.make_async_copy(tgt_hbm, tgt.at[0], load_sem.at[2])]
    for load in loads:
        load.start()

    barrier = pltpu.get_barrier_semaphore()
    for mask in direct:
        pl.semaphore_signal(barrier, inc=1, device_id=(flip(me, mask), rep), device_id_type=MESH)
    for mask in range(1, n_rep):
        pl.semaphore_signal(barrier, inc=1, device_id=(me, flip(rep, mask)), device_id_type=MESH)
    for load in loads:
        load.wait()
    pl.semaphore_wait(barrier, len(direct) + n_rep - 1)

    def send_emb(source, target, to):
        return pltpu.make_async_remote_copy(
            src_ref=emb.at[source, half],
            dst_ref=emb.at[target, half],
            send_sem=emb_send.at[target],
            recv_sem=emb_recv.at[target],
            device_id=(flip(me, to), rep),
            device_id_type=MESH,
        )

    def send_tgt(source, target, to):
        return pltpu.make_async_remote_copy(
            src_ref=tgt.at[source],
            dst_ref=tgt.at[target],
            send_sem=tgt_send.at[target],
            recv_sem=tgt_recv.at[target],
            device_id=(flip(me, to), rep),
            device_id_type=MESH,
        )

    def send_core(at):
        return pltpu.make_async_remote_copy(
            src_ref=emb.at[at, half],
            dst_ref=emb.at[at, half],
            send_sem=core_send.at[at],
            recv_sem=core_recv.at[at],
            device_id=(me, flip(rep, 1)),
            device_id_type=MESH,
        )

    emb_copies, tgt_copies, core_copies = {}, {}, {}
    for mask in direct:
        p = place[mask]
        emb_copies[p] = send_emb(0, p, mask)
        emb_copies[p].start()
    for mask in direct:
        p = place[mask]
        tgt_copies[p] = send_tgt(0, p, mask)
        tgt_copies[p].start()

    def take_emb(p):
        onward = place[masks[p] + 1] if masks[p] in direct[1:] else None
        emb_copies[p].wait_recv()
        if onward is not None:
            emb_copies[onward] = send_emb(p, onward, 1)
            emb_copies[onward].start()
        core_copies[p] = send_core(p)
        core_copies[p].start()

    def take_tgt(p):
        onward = place[masks[p] + 1] if masks[p] in direct[1:] else None
        tgt_copies[p].wait_recv()
        if onward is not None:
            tgt_copies[onward] = send_tgt(p, onward, 1)
            tgt_copies[onward].start()

    def tile(own, own_norm, far, far_norm):
        distance = jnp.maximum((own_norm + far_norm) + dot_nt(own, far), TINY)
        return jnp.exp(-(distance * lax.rsqrt(distance)) / length_scale)

    ones = jnp.ones((8, dim), jnp.bfloat16)

    def build(p):
        here = pl.ds(p * pts, pts)
        points = emb[p].reshape(pts, dim)
        wide = points.astype(jnp.float32)
        squares = wide * wide
        col_norm[here, :] = jnp.sum(squares, axis=1, keepdims=True)
        s_high, s_low = split(squares)
        row_norm[:, here] = dot_nt(ones, s_high) + dot_nt(ones, s_low)
        scaled[here, :] = -2.0 * points
        upto, before = pl.ds(0, (p + 1) * pts), pl.ds(0, p * pts)
        far = emb[0 : p + 1].reshape((p + 1) * pts, dim)
        for_row = tile(scaled[here, :], col_norm[here, :], far, row_norm[0:1, upto])
        diagonal = for_row[:, p * pts :]
        row_id = lax.broadcasted_iota(jnp.int32, (pts, pts), 0)
        col_id = lax.broadcasted_iota(jnp.int32, (pts, pts), 1)
        d_high, d_low = split(jnp.where(row_id == col_id, 1.0, diagonal))
        k_high[here, here] = d_high
        k_low[here, here] = d_low
        if p:
            r_high, r_low = split(for_row[:, : p * pts])
            k_high[here, before] = r_high
            k_low[here, before] = r_low
            k_high[before, here] = r_high.T
            k_low[before, here] = r_low.T

    build(0)
    n_direct = len(direct)

    def add(p):
        core_copies[p].wait_recv()
        build(p)

    for p in range(1, n_direct + 1):
        take_emb(p)
    add(1)
    for p in range(1, n_direct + 1):
        take_tgt(p)
    for p in range(2, n_direct):
        add(p)
    if n_direct + 1 < n_blk:
        take_emb(n_direct + 1)
    add(n_direct)
    for p in range(n_direct + 2, n_blk):
        take_emb(p)
    for p in range(n_direct + 1, n_blk):
        add(p)
    for p in range(n_direct + 1, n_blk):
        take_tgt(p)

    whole = pl.ds(0, n_blk * pts)

    def apply(v):
        v_high, v_low = split(v)
        v_pair[pl.ds(0, rhs), :] = v_high
        v_pair[pl.ds(rhs, rhs), :] = v_low
        return product(v_pair, k_high, k_low, rhs, whole, whole) + noise_var * v

    everything = jnp.concatenate([tgt[p] for p in range(n_blk)], axis=1)
    along = apply(everything)
    rr, pr = fold(everything * everything), fold(everything * along)
    rr_sum = jnp.sum(rr, axis=1, keepdims=True)
    pr_sum = jnp.sum(pr, axis=1, keepdims=True)

    def step_of(norm, prod):
        usable = jnp.logical_and(norm > 0.0, prod > 0.0)
        return jnp.where(usable, norm / jnp.where(usable, prod, 1.0), 1.0)

    local = step_of(rr_sum, pr_sum)
    w = everything - local * along
    aw = apply(w)
    aa = (along - aw) / local
    sums = jnp.concatenate(
        [
            rr,
            pr,
            fold(w * w),
            fold(w * along),
            fold(along * along),
            fold(w * aw),
            fold(w * aa + along * aw),
            fold(along * aa),
        ],
        axis=0,
    )
    parts[0] = jnp.broadcast_to(jnp.sum(sums, axis=1, keepdims=True), parts.shape[1:])
    part_copies = []
    for mask in range(1, n_rep):
        copy = pltpu.make_async_remote_copy(
            src_ref=parts.at[0],
            dst_ref=parts.at[mask],
            send_sem=part_send.at[mask],
            recv_sem=part_recv.at[mask],
            device_id=(me, flip(rep, mask)),
            device_id_type=MESH,
        )
        copy.start()
        part_copies.append(copy)
    for p in range(1, n_blk):
        emb_copies[p].wait_send()
        tgt_copies[p].wait_send()
        core_copies[p].wait_send()
    for copy in part_copies:
        copy.wait()

    tiles = [parts[i] for i in range(n_rep)]
    norm_now = sum(t[0:1] for t in tiles)
    alpha = norm_now / sum(t[1:2] for t in tiles)
    norm_next = jnp.zeros_like(norm_now)
    prod = jnp.zeros_like(norm_now)
    for t in tiles:
        delta = alpha - step_of(t[0:1], t[1:2])
        norm_next = norm_next + (t[2:3] - delta * (2.0 * t[3:4] - delta * t[4:5]))
        prod = prod + (t[5:6] - delta * (t[6:7] - delta * t[7:8]))
    ratio = norm_next / norm_now
    alpha_next = norm_next / (prod - ratio * norm_next / alpha)
    delta = alpha - step_of(tiles[0][0:1], tiles[0][1:2])
    own_t, own_a = everything[:, :pts], along[:, :pts]
    residual = w[:, :pts] - delta * own_a
    image_r = aw[:, :pts] - delta * aa[:, :pts]
    direction = residual + ratio * own_t
    out_ref[0] = alpha * own_t + alpha_next * direction
    out_ref[1] = residual - alpha_next * (image_r + ratio * own_a)


def fused(n_blk, n_rep, embeddings, targets):
    pts, dim = embeddings.shape
    rhs = targets.shape[0]
    total = n_blk * pts
    dma = pltpu.SemaphoreType.DMA
    out = pl.pallas_call(
        functools.partial(kernel, n_blk, n_rep),
        out_shape=jax.ShapeDtypeStruct((2, rhs, pts), jnp.float32),
        in_specs=[pl.BlockSpec(memory_space=pl.ANY)] * 2,
        out_specs=pl.BlockSpec(memory_space=pltpu.VMEM),
        scratch_shapes=[
            pltpu.VMEM((n_blk, 2, pts // 2, dim), jnp.bfloat16),
            pltpu.VMEM((n_blk, rhs, pts), jnp.float32),
            pltpu.VMEM((total, dim), jnp.bfloat16),
            pltpu.VMEM((total, 1), jnp.float32),
            pltpu.VMEM((8, total), jnp.float32),
            pltpu.VMEM((total, total), jnp.bfloat16),
            pltpu.VMEM((total, total), jnp.bfloat16),
            pltpu.VMEM((2 * rhs, total), jnp.bfloat16),
            pltpu.VMEM((n_rep, 8, 128), jnp.float32),
            dma((3,)),
            dma((n_blk,)),
            dma((n_blk,)),
            dma((n_blk,)),
            dma((n_blk,)),
            dma((n_blk,)),
            dma((n_blk,)),
            dma((n_rep,)),
            dma((n_rep,)),
        ],
        compiler_params=pltpu.CompilerParams(collective_id=0, has_side_effects=True),
    )(embeddings, targets)
    return out[0], out[1]


def power_of_two(n):
    return n >= 2 and n & (n - 1) == 0


def fits(n_blk, n_rep, embeddings, targets):
    pts, dim = embeddings.shape
    rhs = targets.shape[0]
    total = n_blk * pts
    return (
        power_of_two(n_blk)
        and power_of_two(n_rep)
        and pts == 128
        and dim % 128 == 0
        and rhs % 16 == 0
        and rhs <= 128
        and total <= 2048
        and dim <= 1024
    )


def squared_norms(points):
    widened = points.astype(jnp.float32)
    return jnp.sum(widened * widened, axis=1)


def kernel_tile(own_points, own_norms, own_labels, far_points, far_norms, far_labels):
    products = jnp.einsum("pd,qd->pq", own_points, far_points, preferred_element_type=jnp.float32)
    distance_sq = own_norms[:, None] + far_norms[None, :] - 2.0 * products
    distance_sq = jnp.where(own_labels[:, None] == far_labels[None, :], 0.0, distance_sq)
    return jnp.exp(-jnp.sqrt(distance_sq) / length_scale)


def paired(residual, image):
    return lax.psum((jnp.sum(residual * residual), jnp.sum(residual * image)), ("blk", "rep"))


def per_device(embeddings, targets):
    block_id = lax.axis_index("blk")
    local_count = embeddings.shape[0]
    own_norms = squared_norms(embeddings)
    own_labels = block_id * local_count + jnp.arange(local_count, dtype=jnp.int32)
    everyone = lax.all_gather(embeddings, "blk", axis=0, tiled=True)
    every_norms = squared_norms(everyone)

    def folded_image(direction):
        piece = lax.all_gather(direction, "blk", axis=1, tiled=True)
        count = piece.shape[1]
        far_labels = jnp.arange(count, dtype=jnp.int32)
        tile = kernel_tile(embeddings, own_norms, own_labels, everyone, every_norms, far_labels)
        total = jnp.einsum(
            "rq,pq->rp",
            piece,
            tile,
            precision=lax.Precision.HIGHEST,
            preferred_element_type=jnp.float32,
        )
        return total + noise_var * direction

    solution = jnp.zeros_like(targets)
    residual = targets
    image = folded_image(residual)
    norm_now, product = paired(residual, image)
    alpha = norm_now / product
    direction = residual
    along = image
    for iteration in range(ITERS):
        solution = solution + alpha * direction
        residual = residual - alpha * along
        if iteration + 1 < ITERS:
            image = folded_image(residual)
            norm_next, product = paired(residual, image)
            ratio = norm_next / norm_now
            alpha = norm_next / (product - ratio * norm_next / alpha)
            direction = residual + ratio * direction
            along = image + ratio * along
            norm_now = norm_next
    return (solution, residual)


def solution(mesh):
    n_blk, n_rep = mesh.shape["blk"], mesh.shape["rep"]

    def step(embeddings, targets):
        if fits(n_blk, n_rep, embeddings, targets):
            return fused(n_blk, n_rep, embeddings, targets)
        return per_device(embeddings, targets)

    in_specs = (P("blk", None), P("rep", "blk"))
    out_specs = (P("rep", "blk"), P("rep", "blk"))
    return jax.shard_map(step, mesh=mesh, in_specs=in_specs, out_specs=out_specs, check_vma=False)
```

```python
import functools

import jax
import jax.numpy as jnp
from jax import lax
from jax.experimental import pallas as pl
from jax.experimental.pallas import tpu as pltpu
from jax.sharding import PartitionSpec as P

ITERS = 2
MESH = pl.DeviceIdType.MESH
TINY = 1e-30

length_scale = 1.0
noise_var = 1.0


def flip(index, mask):
    bit = 1
    while bit <= mask:
        if mask & bit:
            index = index + bit * (1 - 2 * ((index // bit) % 2))
        bit *= 2
    return index


def dot_nt(a, b):
    return lax.dot_general(a, b, (((1,), (1,)), ((), ())), preferred_element_type=jnp.float32)


def split(x):
    high = x.astype(jnp.bfloat16)
    low = (x - high.astype(jnp.float32)).astype(jnp.bfloat16)
    return high, low


def product(v_ref, high_ref, low_ref, rhs, rows, columns):
    both = jnp.dot(v_ref[:, rows], high_ref[rows, columns], preferred_element_type=jnp.float32)
    low = jnp.dot(v_ref[pl.ds(0, rhs), rows], low_ref[rows, columns], preferred_element_type=jnp.float32)
    return both[:rhs] + (both[rhs:] + low)


def fold(x):
    rows = jnp.sum(x, axis=0, keepdims=True)
    total = rows[:, :128]
    for at in range(128, rows.shape[1], 128):
        total = total + rows[:, at : at + 128]
    return total


def kernel(
    n_blk,
    n_rep,
    emb_hbm,
    tgt_hbm,
    out_ref,
    emb,
    tgt,
    scaled,
    col_norm,
    row_norm,
    k_high,
    k_low,
    v_pair,
    parts,
    load_sem,
    emb_send,
    emb_recv,
    tgt_send,
    tgt_recv,
    core_send,
    core_recv,
    part_send,
    part_recv,
):
    pts, dim = emb.shape[2] * 2, emb.shape[3]
    rhs = tgt.shape[1]
    me = lax.axis_index("blk")
    rep = lax.axis_index("rep")
    half = rep % 2
    masks = [0, 1] + list(range(2, n_blk, 2)) + list(range(3, n_blk, 2))
    place = {mask: p for p, mask in enumerate(masks)}
    direct = [1] + list(range(2, n_blk, 2))

    loads = [
        pltpu.make_async_copy(emb_hbm.at[pl.ds(i * (pts // 2), pts // 2)], emb.at[0, i], load_sem.at[i])
        for i in range(2)
    ] + [pltpu.make_async_copy(tgt_hbm, tgt.at[0], load_sem.at[2])]
    for load in loads:
        load.start()

    barrier = pltpu.get_barrier_semaphore()
    for mask in direct:
        pl.semaphore_signal(barrier, inc=1, device_id=(flip(me, mask), rep), device_id_type=MESH)
    for mask in range(1, n_rep):
        pl.semaphore_signal(barrier, inc=1, device_id=(me, flip(rep, mask)), device_id_type=MESH)
    for load in loads:
        load.wait()
    pl.semaphore_wait(barrier, len(direct) + n_rep - 1)

    def send_emb(source, target, to):
        return pltpu.make_async_remote_copy(
            src_ref=emb.at[source, half],
            dst_ref=emb.at[target, half],
            send_sem=emb_send.at[target],
            recv_sem=emb_recv.at[target],
            device_id=(flip(me, to), rep),
            device_id_type=MESH,
        )

    def send_tgt(source, target, to):
        return pltpu.make_async_remote_copy(
            src_ref=tgt.at[source],
            dst_ref=tgt.at[target],
            send_sem=tgt_send.at[target],
            recv_sem=tgt_recv.at[target],
            device_id=(flip(me, to), rep),
            device_id_type=MESH,
        )

    def send_core(at):
        return pltpu.make_async_remote_copy(
            src_ref=emb.at[at, half],
            dst_ref=emb.at[at, half],
            send_sem=core_send.at[at],
            recv_sem=core_recv.at[at],
            device_id=(me, flip(rep, 1)),
            device_id_type=MESH,
        )

    emb_copies, tgt_copies, core_copies = {}, {}, {}
    for mask in direct:
        p = place[mask]
        emb_copies[p] = send_emb(0, p, mask)
        emb_copies[p].start()
    for mask in direct:
        p = place[mask]
        tgt_copies[p] = send_tgt(0, p, mask)
        tgt_copies[p].start()

    def take_emb(p):
        onward = place[masks[p] + 1] if masks[p] in direct[1:] else None
        emb_copies[p].wait_recv()
        if onward is not None:
            emb_copies[onward] = send_emb(p, onward, 1)
            emb_copies[onward].start()
        core_copies[p] = send_core(p)
        core_copies[p].start()

    def take_tgt(p):
        onward = place[masks[p] + 1] if masks[p] in direct[1:] else None
        tgt_copies[p].wait_recv()
        if onward is not None:
            tgt_copies[onward] = send_tgt(p, onward, 1)
            tgt_copies[onward].start()

    def tile(own, own_norm, far, far_norm):
        distance = jnp.maximum((own_norm + far_norm) + dot_nt(own, far), TINY)
        return jnp.exp(-(distance * lax.rsqrt(distance)) / length_scale)

    ones = jnp.ones((8, dim), jnp.bfloat16)

    def build(p):
        here = pl.ds(p * pts, pts)
        points = emb[p].reshape(pts, dim)
        wide = points.astype(jnp.float32)
        squares = wide * wide
        col_norm[here, :] = jnp.sum(squares, axis=1, keepdims=True)
        s_high, s_low = split(squares)
        row_norm[:, here] = dot_nt(ones, s_high) + dot_nt(ones, s_low)
        scaled[here, :] = -2.0 * points
        upto, before = pl.ds(0, (p + 1) * pts), pl.ds(0, p * pts)
        far = emb[0 : p + 1].reshape((p + 1) * pts, dim)
        for_row = tile(scaled[here, :], col_norm[here, :], far, row_norm[0:1, upto])
        diagonal = for_row[:, p * pts :]
        row_id = lax.broadcasted_iota(jnp.int32, (pts, pts), 0)
        col_id = lax.broadcasted_iota(jnp.int32, (pts, pts), 1)
        d_high, d_low = split(jnp.where(row_id == col_id, 1.0, diagonal))
        k_high[here, here] = d_high
        k_low[here, here] = d_low
        if p:
            r_high, r_low = split(for_row[:, : p * pts])
            k_high[here, before] = r_high
            k_low[here, before] = r_low
            k_high[before, here] = r_high.T
            k_low[before, here] = r_low.T

    build(0)
    n_direct = len(direct)

    def add(p):
        core_copies[p].wait_recv()
        build(p)

    for p in range(1, n_direct + 1):
        take_emb(p)
    add(1)
    for p in range(1, n_direct + 1):
        take_tgt(p)
    for p in range(2, n_direct):
        add(p)
    if n_direct + 1 < n_blk:
        take_emb(n_direct + 1)
    add(n_direct)
    for p in range(n_direct + 2, n_blk):
        take_emb(p)
        add(p - 1)
    add(n_blk - 1)
    for p in range(n_direct + 1, n_blk):
        take_tgt(p)

    whole = pl.ds(0, n_blk * pts)

    def apply(v):
        v_high, v_low = split(v)
        v_pair[pl.ds(0, rhs), :] = v_high
        v_pair[pl.ds(rhs, rhs), :] = v_low
        return product(v_pair, k_high, k_low, rhs, whole, whole) + noise_var * v

    everything = jnp.concatenate([tgt[p] for p in range(n_blk)], axis=1)
    along = apply(everything)
    rr, pr = fold(everything * everything), fold(everything * along)
    rr_sum = jnp.sum(rr, axis=1, keepdims=True)
    pr_sum = jnp.sum(pr, axis=1, keepdims=True)

    def step_of(norm, prod):
        usable = jnp.logical_and(norm > 0.0, prod > 0.0)
        return jnp.where(usable, norm / jnp.where(usable, prod, 1.0), 1.0)

    local = step_of(rr_sum, pr_sum)
    w = everything - local * along
    aw = apply(w)
    aa = (along - aw) / local
    sums = jnp.concatenate(
        [
            rr,
            pr,
            fold(w * w),
            fold(w * along),
            fold(along * along),
            fold(w * aw),
            fold(w * aa + along * aw),
            fold(along * aa),
        ],
        axis=0,
    )
    parts[0] = jnp.broadcast_to(jnp.sum(sums, axis=1, keepdims=True), parts.shape[1:])
    part_copies = []
    for mask in range(1, n_rep):
        copy = pltpu.make_async_remote_copy(
            src_ref=parts.at[0],
            dst_ref=parts.at[mask],
            send_sem=part_send.at[mask],
            recv_sem=part_recv.at[mask],
            device_id=(me, flip(rep, mask)),
            device_id_type=MESH,
        )
        copy.start()
        part_copies.append(copy)
    for p in range(1, n_blk):
        emb_copies[p].wait_send()
        tgt_copies[p].wait_send()
        core_copies[p].wait_send()
    for copy in part_copies:
        copy.wait()

    tiles = [parts[i] for i in range(n_rep)]
    norm_now = sum(t[0:1] for t in tiles)
    alpha = norm_now / sum(t[1:2] for t in tiles)
    norm_next = jnp.zeros_like(norm_now)
    prod = jnp.zeros_like(norm_now)
    for t in tiles:
        delta = alpha - step_of(t[0:1], t[1:2])
        norm_next = norm_next + (t[2:3] - delta * (2.0 * t[3:4] - delta * t[4:5]))
        prod = prod + (t[5:6] - delta * (t[6:7] - delta * t[7:8]))
    ratio = norm_next / norm_now
    alpha_next = norm_next / (prod - ratio * norm_next / alpha)
    delta = alpha - step_of(tiles[0][0:1], tiles[0][1:2])
    own_t, own_a = everything[:, :pts], along[:, :pts]
    residual = w[:, :pts] - delta * own_a
    image_r = aw[:, :pts] - delta * aa[:, :pts]
    direction = residual + ratio * own_t
    out_ref[0] = alpha * own_t + alpha_next * direction
    out_ref[1] = residual - alpha_next * (image_r + ratio * own_a)


def fused(n_blk, n_rep, embeddings, targets):
    pts, dim = embeddings.shape
    rhs = targets.shape[0]
    total = n_blk * pts
    dma = pltpu.SemaphoreType.DMA
    out = pl.pallas_call(
        functools.partial(kernel, n_blk, n_rep),
        out_shape=jax.ShapeDtypeStruct((2, rhs, pts), jnp.float32),
        in_specs=[pl.BlockSpec(memory_space=pl.ANY)] * 2,
        out_specs=pl.BlockSpec(memory_space=pltpu.VMEM),
        scratch_shapes=[
            pltpu.VMEM((n_blk, 2, pts // 2, dim), jnp.bfloat16),
            pltpu.VMEM((n_blk, rhs, pts), jnp.float32),
            pltpu.VMEM((total, dim), jnp.bfloat16),
            pltpu.VMEM((total, 1), jnp.float32),
            pltpu.VMEM((8, total), jnp.float32),
            pltpu.VMEM((total, total), jnp.bfloat16),
            pltpu.VMEM((total, total), jnp.bfloat16),
            pltpu.VMEM((2 * rhs, total), jnp.bfloat16),
            pltpu.VMEM((n_rep, 8, 128), jnp.float32),
            dma((3,)),
            dma((n_blk,)),
            dma((n_blk,)),
            dma((n_blk,)),
            dma((n_blk,)),
            dma((n_blk,)),
            dma((n_blk,)),
            dma((n_rep,)),
            dma((n_rep,)),
        ],
        compiler_params=pltpu.CompilerParams(collective_id=0, has_side_effects=True),
    )(embeddings, targets)
    return out[0], out[1]


def power_of_two(n):
    return n >= 2 and n & (n - 1) == 0


def fits(n_blk, n_rep, embeddings, targets):
    pts, dim = embeddings.shape
    rhs = targets.shape[0]
    total = n_blk * pts
    return (
        power_of_two(n_blk)
        and power_of_two(n_rep)
        and pts == 128
        and dim % 128 == 0
        and rhs % 16 == 0
        and rhs <= 128
        and total <= 2048
        and dim <= 1024
    )


def squared_norms(points):
    widened = points.astype(jnp.float32)
    return jnp.sum(widened * widened, axis=1)


def kernel_tile(own_points, own_norms, own_labels, far_points, far_norms, far_labels):
    products = jnp.einsum("pd,qd->pq", own_points, far_points, preferred_element_type=jnp.float32)
    distance_sq = own_norms[:, None] + far_norms[None, :] - 2.0 * products
    distance_sq = jnp.where(own_labels[:, None] == far_labels[None, :], 0.0, distance_sq)
    return jnp.exp(-jnp.sqrt(distance_sq) / length_scale)


def paired(residual, image):
    return lax.psum((jnp.sum(residual * residual), jnp.sum(residual * image)), ("blk", "rep"))


def per_device(embeddings, targets):
    block_id = lax.axis_index("blk")
    local_count = embeddings.shape[0]
    own_norms = squared_norms(embeddings)
    own_labels = block_id * local_count + jnp.arange(local_count, dtype=jnp.int32)
    everyone = lax.all_gather(embeddings, "blk", axis=0, tiled=True)
    every_norms = squared_norms(everyone)

    def folded_image(direction):
        piece = lax.all_gather(direction, "blk", axis=1, tiled=True)
        count = piece.shape[1]
        far_labels = jnp.arange(count, dtype=jnp.int32)
        tile = kernel_tile(embeddings, own_norms, own_labels, everyone, every_norms, far_labels)
        total = jnp.einsum(
            "rq,pq->rp",
            piece,
            tile,
            precision=lax.Precision.HIGHEST,
            preferred_element_type=jnp.float32,
        )
        return total + noise_var * direction

    solution = jnp.zeros_like(targets)
    residual = targets
    image = folded_image(residual)
    norm_now, product = paired(residual, image)
    alpha = norm_now / product
    direction = residual
    along = image
    for iteration in range(ITERS):
        solution = solution + alpha * direction
        residual = residual - alpha * along
        if iteration + 1 < ITERS:
            image = folded_image(residual)
            norm_next, product = paired(residual, image)
            ratio = norm_next / norm_now
            alpha = norm_next / (product - ratio * norm_next / alpha)
            direction = residual + ratio * direction
            along = image + ratio * along
            norm_now = norm_next
    return (solution, residual)


def solution(mesh):
    n_blk, n_rep = mesh.shape["blk"], mesh.shape["rep"]

    def step(embeddings, targets):
        if fits(n_blk, n_rep, embeddings, targets):
            return fused(n_blk, n_rep, embeddings, targets)
        return per_device(embeddings, targets)

    in_specs = (P("blk", None), P("rep", "blk"))
    out_specs = (P("rep", "blk"), P("rep", "blk"))
    return jax.shard_map(step, mesh=mesh, in_specs=in_specs, out_specs=out_specs, check_vma=False)
```
